32 devices in a mesh: rows: 16 (over z, x, core), heads: 2 (over y).
Axes of the slice: x: 2, y: 2, z: 4, core: 2. Of those that a mesh axis runs over, the one named last changes fastest.
Arguments:
- queries: bfloat16 [32, 4, 32, 1024], P('rows', 'heads'), may hold values from -6 to 6
- keys: bfloat16 [32, 4, 32, 1024], P('rows', 'heads'), may hold values from -6 to 6
- values: bfloat16 [32, 4, 32, 1024], P('rows', 'heads'), may hold values from -6 to 6
- d_out: bfloat16 [32, 4, 32, 1024], P('rows', 'heads'), may hold values from -8 to 8
- bias: bfloat16 [4, 1024, 1024], P('heads', 'rows'), may hold values from -4 to 400, as said below
- w_bias: bfloat16 [128, 4], replicated, may hold values from -96 to 96
Outputs:
- d_queries: bfloat16 [32, 4, 32, 1024], P('rows', 'heads')
- d_keys: bfloat16 [32, 4, 32, 1024], P('rows', 'heads')
- d_values: bfloat16 [32, 4, 32, 1024], P('rows', 'heads')
- d_pair: bfloat16 [1024, 1024, 128], P('rows', 'heads')
The draws below stay inside these ranges and needn't reach their ends.
Inputs may be any that keep to these rules, and one draw needn't show every extreme that they name: bias entries stay within the stated bounds.
All inputs are finite; a program needn't handle non-finite values.
Results may differ from the reference program's by a relative error of at most 0.0051.
Values may be sent and summed in bfloat16 or wider, within the bound.
A program may use at most 64 MiB of HBM per device.

```python
import jax
import jax.numpy as jnp
from jax import lax

C = 128
H = 4
D = 32
L = 1024
ROWS = 32


def draw_bias(key, part):
    key_base = jax.random.fold_in(key, 11)
    base = jnp.clip(jax.random.normal(key_base, (H, L, L), jnp.float32), -4.0, 4.0)
    return base.astype(jnp.bfloat16)


def with_spikes(entries, own_key, source, target, blocks, factor):
    def block_of(axis_at):
        return (jnp.arange(entries.shape[axis_at]) // (entries.shape[axis_at] // blocks)).reshape((-1,) + (1,) * (entries.ndim - 1 - axis_at))

    near = jax.random.permutation(own_key, blocks)[block_of(target)]
    second = (block_of(target) + blocks // 2) % blocks
    return jnp.where((block_of(source) == near) | (block_of(source) == second), factor * entries, entries)


def shard_levels(rng, dims, cuts, low, high):
    level = 1.0
    for position, shards_of in cuts:
        draws = jax.random.uniform(jax.random.fold_in(jax.random.fold_in(rng, 6), position), (shards_of,), jnp.float32, low / len(cuts), high / len(cuts))
        level = level * jnp.repeat(jnp.exp(draws), dims[position] // shards_of).reshape((-1,) + (1,) * (len(dims) - 1 - position))
    return level


def bell_draw(own_key, extent, width, bound, pieces=(), dtype=jnp.bfloat16):
    entries = jax.random.normal(own_key, extent, jnp.float32) * width
    if len(pieces) > 0:
        entries = shard_levels(own_key, extent, pieces, -0.22, 0.18) * entries
    return jnp.clip(entries, min=-bound, max=bound).astype(dtype)


def heavy_noise(own_key, shape, scale, most, cuts, heavy, dtype=jnp.bfloat16):
    drawn = scale * jax.random.normal(own_key, shape, jnp.float32)
    if cuts:
        drawn = drawn * shard_levels(own_key, shape, cuts, -0.22, 0.18)
    return jnp.clip(with_spikes(drawn, jax.random.fold_in(own_key, 3), *heavy), -most, most).astype(dtype)


def setup_inputs(seed: int = 0) -> dict:
    key_of = jax.random.split(jax.random.key(seed), 7)
    return {
        "queries": bell_draw(key_of[0], (ROWS, H, D, L), 1.0, 6.0, ((0, 16), (1, 2))),
        "keys": bell_draw(key_of[1], (ROWS, H, D, L), 1.0, 6.0, ((0, 16), (1, 2))),
        "values": bell_draw(key_of[2], (ROWS, H, D, L), 1.0, 6.0, ((0, 16), (1, 2))),
        "d_out": heavy_noise(key_of[3], (ROWS, H, D, L), 1.0, 8.0, ((0, 16), (1, 2)), (0, 3, 16, 2.0)),
        "bias": draw_bias(jax.random.fold_in(key_of[6], 71), 0),
        "w_bias": bell_draw(key_of[5], (C, H), 16.0, 96.0),
    }


def reference(queries, keys, values, d_out, bias, w_bias):
    scale = D ** -0.5
    bias_f = bias.astype(jnp.float32)

    def step(d_bias, items):
        q_row, k_row, v_row, g_row = [t.astype(jnp.float32) for t in items]
        scores = jnp.einsum('hdq,hdk->hqk', q_row, k_row) * scale + bias_f
        top = jnp.max(scores, axis=-1, keepdims=True)
        expo = jnp.exp(scores - top)
        probs = expo / jnp.sum(expo, axis=-1, keepdims=True)
        d_probs = jnp.einsum('hdq,hdk->hqk', g_row, v_row)
        d_scores = probs * (d_probs - jnp.sum(probs * d_probs, axis=-1, keepdims=True))
        probs_low = lax.optimization_barrier(probs.astype(jnp.bfloat16)).astype(jnp.float32)
        d_low = lax.optimization_barrier(d_scores.astype(jnp.bfloat16)).astype(jnp.float32)
        grad_q = jnp.einsum('hqk,hdk->hdq', d_low, k_row) * scale
        grad_k = jnp.einsum('hqk,hdq->hdk', d_low, q_row) * scale
        grad_v = jnp.einsum('hqk,hdq->hdk', probs_low, g_row)
        return d_bias + d_scores, (grad_q.astype(jnp.bfloat16), grad_k.astype(jnp.bfloat16), grad_v.astype(jnp.bfloat16))

    start_bias = jnp.zeros((H, L, L), jnp.float32)
    d_bias, grads = lax.scan(step, start_bias, (queries, keys, values, d_out))
    d_pair = jnp.einsum('hjk,ch->jkc', d_bias, w_bias.astype(jnp.float32), precision=lax.Precision.HIGHEST)
    return grads[0], grads[1], grads[2], d_pair.astype(jnp.bfloat16)
```

```python
import functools

import jax
import jax.numpy as jnp
from jax import lax
from jax.experimental import pallas as pl
from jax.experimental.pallas import tpu as pltpu
from jax.sharding import PartitionSpec as P

MESH = pl.DeviceIdType.MESH
GROUP = 4
BF16, F32 = jnp.bfloat16, jnp.float32


def xor(a, b, top):
    total, bit = 0, 1
    while bit < top:
        total = total + bit * lax.rem(lax.rem(lax.div(a, bit), 2) + lax.rem(lax.div(b, bit), 2), 2)
        bit *= 2
    return total


def attention_kernel(
    n, nh, q_ref, k_ref, v_ref, g_ref, bias_ref, dq_ref, dk_ref, dv_ref, eh_ref,
    q_t, g_t, k_t, dq_t, dk_acc, dv_acc, p_low, d_low, d_blk,
    bias_all, core_send, core_keep, core_recv, side_send, side_keep, side_recv,
    far_send, far_recv, own, fin, y_recv,
    zs, zr, xs, xr, as_, ar, bs, br, cs, cr, ss, sr, fs, fr, ys, yr,
):
    rows, heads, depth, length = q_ref.shape
    j_own = length // n
    blocks = n // GROUP
    steps = heads * blocks
    width = length // nh
    scale = depth ** (-0.5)
    me, hd = lax.axis_index("rows"), lax.axis_index("heads")
    core = lax.rem(me, 2)
    side = lax.rem(lax.div(me, 2), 2)
    far = lax.div(me, GROUP)
    core_peer = (me + 1 - 2 * core, hd)
    side_peer = (me + 2 - 4 * side, hd)

    def far_peer(i):
        return (xor(far, i, blocks) * GROUP + lax.rem(me, GROUP), hd)

    def step_of(t):
        h = lax.div(t, blocks)
        i = lax.rem(t, blocks)
        return h, i + lax.rem(h, 2) * (blocks - 1 - 2 * i)

    def remote(src, dst, send, recv, device):
        return pltpu.make_async_remote_copy(
            src_ref=src, dst_ref=dst, send_sem=send, recv_sem=recv, device_id=device, device_id_type=MESH
        )

    def bias_far(h, i):
        return remote(bias_ref.at[h], bias_all.at[h, i, side, core], zs.at[h, i], zr.at[h, i], far_peer(i))

    def bias_side(h, i):
        spot = bias_all.at[h, i, side, core]
        return remote(spot, spot, xs.at[h, i], xr.at[h, i], side_peer)

    def bias_core_a(h, i):
        spot = bias_all.at[h, i, side, core]
        return remote(spot, spot, as_.at[h, i], ar.at[h, i], core_peer)

    def bias_core_b(h, i):
        spot = bias_all.at[h, i, 1 - side, core]
        return remote(spot, spot, bs.at[h, i], br.at[h, i], core_peer)

    def sum_core(t):
        return remote(core_send.at[t], core_recv.at[t], cs.at[t], cr.at[t], core_peer)

    def sum_side(t):
        return remote(side_send.at[t], side_recv.at[t], ss.at[t], sr.at[t], side_peer)

    def sum_far(h, i):
        return remote(far_send.at[h, i], far_recv.at[h, i], fs.at[h, i], fr.at[h, i], far_peer(i))

    def head_copy(o, h):
        to = lax.rem(hd + o, nh)
        return remote(fin.at[to, h], y_recv.at[o - 1, h], ys.at[o - 1, h], yr.at[o - 1, h], (me, to))

    def stage_far(t):
        h, i = step_of(t)

        @pl.when(i != 0)
        def _():
            bias_far(h, i).wait_recv()

        bias_side(h, i).start()
        bias_core_a(h, i).start()

    def stage_side(t):
        h, i = step_of(t)
        bias_side(h, i).wait_recv()
        bias_core_b(h, i).start()

    def stage_core(t):
        h, i = step_of(t)
        bias_core_a(h, i).wait_recv()
        bias_core_b(h, i).wait_recv()

    def reduce_core(t):
        sum_core(t).wait_recv()
        side_send[t] = (core_keep[t, 1 - side] + core_recv[t, 1 - side].astype(F32)).astype(BF16)
        sum_side(t).start()
        side_keep[t] = core_keep[t, side] + core_recv[t, side].astype(F32)

    def reduce_side(t):
        h, i = step_of(t)
        sum_side(t).wait_recv()
        total = side_keep[t] + side_recv[t].astype(F32)

        @pl.when(i != 0)
        def _():
            far_send[h, i] = total.astype(BF16)
            sum_far(h, i).start()

        @pl.when(i == 0)
        def _():
            own[h] = total

    barrier = pltpu.get_barrier_semaphore()
    peers = [core_peer, side_peer]
    peers += [far_peer(i) for i in range(1, blocks)]
    peers += [(me, lax.rem(hd + o, nh)) for o in range(1, nh)]
    for peer in peers:
        pl.semaphore_signal(barrier, inc=1, device_id=peer, device_id_type=MESH)
    pl.semaphore_wait(barrier, len(peers))

    for h in range(heads):
        bias_all[h, 0, side, core] = bias_ref[h]
    stage_far(0)

    @pl.loop(0, steps)
    def _(t):
        h, i = step_of(t)

        @pl.when(i != 0)
        def _():
            bias_far(h, i).start()

    for r in range(rows):
        for h in range(heads):
            q_t[r, h] = q_ref[r, h].T
            g_t[r, h] = g_ref[r, h].T
            k_t[r, h] = k_ref[r, h].T
    dk_acc[...] = jnp.zeros_like(dk_acc)
    dv_acc[...] = jnp.zeros_like(dv_acc)
    stage_side(0)
    if steps > 1:
        stage_far(1)

    block = GROUP * j_own
    sub = min(block, 64)
    per_sub = sub // j_own if sub > j_own else 1
    sub = per_sub * j_own
    nn = (((1,), (0,)), ((), ()))
    tn = (((0,), (0,)), ((), ()))

    @pl.loop(0, steps)
    def _(t):
        h, i = step_of(t)

        @pl.when(t + 2 < steps)
        def _():
            stage_far(t + 2)

        @pl.when(t + 1 < steps)
        def _():
            stage_side(t + 1)

        stage_core(t)
        first = pl.multiple_of(xor(far, i, blocks) * block, block)

        @pl.loop(0, block // sub)
        def _(part):
            at = pl.multiple_of(part * sub, sub)
            pieces = []
            for u in range(per_sub):
                o = part * per_sub + u
                pieces.append(bias_all[h, i, lax.div(o, 2), lax.rem(o, 2)].astype(F32))
            b = pieces[0] if per_sub == 1 else jnp.concatenate(pieces, axis=0)
            total = None
            for r in range(rows):
                qb = q_t[r, h, pl.ds(first + at, sub), :]
                gb = g_t[r, h, pl.ds(first + at, sub), :]
                s = lax.dot_general(qb, k_ref[r, h], nn, preferred_element_type=F32) * scale + b
                e = jnp.exp(s - jnp.max(s, axis=-1, keepdims=True))
                inv = 1.0 / jnp.sum(e, axis=-1, keepdims=True)
                dp = lax.dot_general(gb, v_ref[r, h], nn, preferred_element_type=F32)
                p = e * inv
                delta = jnp.sum(p * dp, axis=-1, keepdims=True)
                ds = p * (dp - delta)
                p_low[r, pl.ds(at, sub), :] = p.astype(BF16)
                d_low[r, pl.ds(at, sub), :] = ds.astype(BF16)
                total = ds if total is None else total + ds
            for u in range(per_sub):
                o = part * per_sub + u
                d_blk[lax.div(o, 2), lax.rem(o, 2)] = total[u * j_own : (u + 1) * j_own]

        core_send[t] = d_blk[:, 1 - core].astype(BF16)
        sum_core(t).start()
        core_keep[t] = d_blk[:, core]
        for r in range(rows):
            qb = q_t[r, h, pl.ds(first, block), :]
            gb = g_t[r, h, pl.ds(first, block), :]
            dq_t[r, h, pl.ds(first, block), :] = lax.dot_general(d_low[r], k_t[r, h], nn, preferred_element_type=F32)
            dk_acc[r, h] += lax.dot_general(qb, d_low[r], tn, preferred_element_type=F32)
            dv_acc[r, h] += lax.dot_general(gb, p_low[r], tn, preferred_element_type=F32)

        @pl.when(t >= 1)
        def _():
            reduce_core(t - 1)

        @pl.when(t >= 2)
        def _():
            reduce_side(t - 2)

    def finish(h):
        @pl.loop(1, blocks)
        def _(i):
            sum_far(h, i).wait_recv()
            own[h] += far_recv[h, i].astype(F32)

        for y in range(nh):
            fin[y, h] = own[h, :, y * width : (y + 1) * width]
        for o in range(1, nh):
            head_copy(o, h).start()
        eh_ref[hd * heads + h] = fin[hd, h]

    reduce_core(steps - 1)
    if steps > 1:
        reduce_side(steps - 2)
    for h in range(heads - 1):
        finish(h)
    for r in range(rows):
        for h in range(heads):
            dq_ref[r, h] = (dq_t[r, h] * scale).T.astype(BF16)
            dk_ref[r, h] = (dk_acc[r, h] * scale).astype(BF16)
            dv_ref[r, h] = dv_acc[r, h].astype(BF16)
    reduce_side(steps - 1)
    finish(heads - 1)
    for h in range(heads):
        for o in range(1, nh):
            copy = head_copy(o, h)
            copy.wait_recv()
            eh_ref[lax.rem(hd + nh - o, nh) * heads + h] = y_recv[o - 1, h]
            copy.wait_send()

    @pl.loop(0, steps)
    def _(t):
        h, i = step_of(t)
        bias_side(h, i).wait_send()
        bias_core_a(h, i).wait_send()
        bias_core_b(h, i).wait_send()
        sum_core(t).wait_send()
        sum_side(t).wait_send()

        @pl.when(i != 0)
        def _():
            bias_far(h, i).wait_send()
            sum_far(h, i).wait_send()


def attention(n, nh, q, k, v, g, bias):
    rows, heads, depth, length = q.shape
    j_own = length // n
    blocks = n // GROUP
    steps = heads * blocks
    block = GROUP * j_own
    width = length // nh
    dma = pltpu.SemaphoreType.DMA
    vm = pltpu.VMEM
    grid2 = (heads, blocks)
    return pl.pallas_call(
        functools.partial(attention_kernel, n, nh),
        out_shape=[jax.ShapeDtypeStruct(q.shape, BF16)] * 3
        + [jax.ShapeDtypeStruct((nh * heads, j_own, width), F32)],
        in_specs=[pl.BlockSpec(memory_space=pltpu.VMEM)] * 5,
        out_specs=[pl.BlockSpec(memory_space=pltpu.VMEM)] * 4,
        scratch_shapes=[
            vm((rows, heads, length, depth), BF16),
            vm((rows, heads, length, depth), BF16),
            vm((rows, heads, length, depth), BF16),
            vm((rows, heads, length, depth), F32),
            vm(q.shape, F32),
            vm(q.shape, F32),
            vm((rows, block, length), BF16),
            vm((rows, block, length), BF16),
            vm((2, 2, j_own, length), F32),
            vm(grid2 + (2, 2, j_own, length), BF16),
            vm((steps, 2, j_own, length), BF16),
            vm((steps, 2, j_own, length), F32),
            vm((steps, 2, j_own, length), BF16),
            vm((steps, j_own, length), BF16),
            vm((steps, j_own, length), F32),
            vm((steps, j_own, length), BF16),
            vm(grid2 + (j_own, length), BF16),
            vm(grid2 + (j_own, length), BF16),
            vm((heads, j_own, length), F32),
            vm((nh, heads, j_own, width), F32),
            vm((max(nh - 1, 1), heads, j_own, width), F32),
        ]
        + [dma(grid2)] * 8
        + [dma((steps,))] * 4
        + [dma(grid2)] * 2
        + [dma((max(nh - 1, 1), heads))] * 2,
        compiler_params=pltpu.CompilerParams(
            collective_id=0, has_side_effects=True, vmem_limit_bytes=56 * 1024 * 1024
        ),
        name="attention",
    )(q, k, v, g, bias)


def pair_kernel(d_ref, w_ref, out_ref):
    heads, count, width = d_ref.shape
    d = d_ref[...].reshape(heads * count, width)
    high = d.astype(BF16)
    rest = d - high.astype(F32)
    mid = rest.astype(BF16)
    low = (rest - mid.astype(F32)).astype(BF16)
    parts = jnp.concatenate([high, mid, low], axis=0)
    channels = out_ref.shape[2]
    res = lax.dot_general(parts, w_ref[...], (((0,), (0,)), ((), ())), preferred_element_type=F32)
    for j in range(count):
        out_ref[j] = res[:, j * channels : (j + 1) * channels].astype(BF16)


def pair(every_head, w_bias):
    heads, j_own, width = every_head.shape
    channels = w_bias.shape[0]
    count = 8
    eye = jnp.eye(count, dtype=BF16)
    wide = (w_bias.T[:, None, None, :] * eye[None, :, :, None]).reshape(heads * count, count * channels)
    wide = jnp.concatenate([wide] * 3, axis=0)
    return pl.pallas_call(
        pair_kernel,
        grid=(j_own // count,),
        in_specs=[
            pl.BlockSpec((heads, count, width), lambda i: (0, i, 0)),
            pl.BlockSpec(wide.shape, lambda i: (0, 0)),
        ],
        out_specs=pl.BlockSpec((count, width, channels), lambda i: (i, 0, 0)),
        out_shape=jax.ShapeDtypeStruct((j_own, width, channels), BF16),
        name="pair",
    )(every_head, wide)


def solution(mesh):
    n, nh = mesh.shape["rows"], mesh.shape["heads"]

    def shards(queries, keys, values, d_out, bias, w_bias):
        dq, dk, dv, every_head = attention(n, nh, queries, keys, values, d_out, bias)
        return dq, dk, dv, pair(every_head, w_bias)

    spec = P("rows", "heads", None, None)
    return jax.shard_map(
        shards,
        mesh=mesh,
        in_specs=(spec, spec, spec, spec, P("heads", "rows", None), P()),
        out_specs=(spec, spec, spec, P("rows", "heads", None)),
        check_vma=False,
    )
```

```python
import functools

import jax
import jax.numpy as jnp
from jax import lax
from jax.experimental import pallas as pl
from jax.experimental.pallas import tpu as pltpu
from jax.sharding import PartitionSpec as P

MESH = pl.DeviceIdType.MESH
AHEAD = 4
GROUP = 4
BF16, F32 = jnp.bfloat16, jnp.float32


def xor(a, b, top):
    total, bit = 0, 1
    while bit < top:
        total = total + bit * lax.rem(lax.rem(lax.div(a, bit), 2) + lax.rem(lax.div(b, bit), 2), 2)
        bit *= 2
    return total


def attention_kernel(
    n, nh, q_ref, k_ref, v_ref, g_ref, bias_ref, dq_ref, dk_ref, dv_ref, eh_ref,
    q_t, g_t, k_t, dq_t, dk_acc, dv_acc, p_low, d_low, d_blk,
    bias_all, core_send, core_keep, core_recv, side_send, side_keep, side_recv,
    far_send, far_recv, own, fin, fin_low, y_recv,
    zs, zr, xs, xr, as_, ar, bs, br, cs, cr, ss, sr, fs, fr, ys, yr,
):
    rows, heads, depth, length = q_ref.shape
    j_own = length // n
    blocks = n // GROUP
    steps = heads * blocks
    width = length // nh
    scale = depth ** (-0.5)
    me, hd = lax.axis_index("rows"), lax.axis_index("heads")
    core = lax.rem(me, 2)
    side = lax.rem(lax.div(me, 2), 2)
    far = lax.div(me, GROUP)
    core_peer = (me + 1 - 2 * core, hd)
    side_peer = (me + 2 - 4 * side, hd)

    def far_peer(i):
        return (xor(far, i, blocks) * GROUP + lax.rem(me, GROUP), hd)

    def step_of(t):
        h = lax.div(t, blocks)
        i = lax.rem(t, blocks)
        return h, i + lax.rem(h, 2) * (blocks - 1 - 2 * i)

    def remote(src, dst, send, recv, device):
        return pltpu.make_async_remote_copy(
            src_ref=src, dst_ref=dst, send_sem=send, recv_sem=recv, device_id=device, device_id_type=MESH
        )

    def bias_far(h, i):
        return remote(bias_ref.at[h], bias_all.at[h, i, side, core], zs.at[h, i], zr.at[h, i], far_peer(i))

    def bias_side(h, i):
        spot = bias_all.at[h, i, side, core]
        return remote(spot, spot, xs.at[h, i], xr.at[h, i], side_peer)

    def bias_core_a(h, i):
        spot = bias_all.at[h, i, side, core]
        return remote(spot, spot, as_.at[h, i], ar.at[h, i], core_peer)

    def bias_core_b(h, i):
        spot = bias_all.at[h, i, 1 - side, core]
        return remote(spot, spot, bs.at[h, i], br.at[h, i], core_peer)

    def sum_core(t):
        return remote(core_send.at[t], core_recv.at[t], cs.at[t], cr.at[t], core_peer)

    def sum_side(t):
        return remote(side_send.at[t], side_recv.at[t], ss.at[t], sr.at[t], side_peer)

    def sum_far(h, i):
        return remote(far_send.at[h, i], far_recv.at[h, i], fs.at[h, i], fr.at[h, i], far_peer(i))

    def head_copy(o, h):
        to = lax.rem(hd + o, nh)
        return remote(fin_low.at[to, h], y_recv.at[o - 1, h], ys.at[o - 1, h], yr.at[o - 1, h], (me, to))

    def stage_far(t):
        h, i = step_of(t)

        @pl.when(i != 0)
        def _():
            bias_far(h, i).wait_recv()

        bias_side(h, i).start()
        bias_core_a(h, i).start()

    def stage_side(t):
        h, i = step_of(t)
        bias_side(h, i).wait_recv()
        bias_core_b(h, i).start()

    def stage_core(t):
        h, i = step_of(t)
        bias_core_a(h, i).wait_recv()
        bias_core_b(h, i).wait_recv()

    def reduce_core(t):
        sum_core(t).wait_recv()
        side_send[t] = (core_keep[t, 1 - side] + core_recv[t, 1 - side].astype(F32)).astype(BF16)
        sum_side(t).start()
        side_keep[t] = core_keep[t, side] + core_recv[t, side].astype(F32)

    def reduce_side(t):
        h, i = step_of(t)
        sum_side(t).wait_recv()
        total = side_keep[t] + side_recv[t].astype(F32)

        @pl.when(i != 0)
        def _():
            far_send[h, i] = total.astype(BF16)
            sum_far(h, i).start()

        @pl.when(i == 0)
        def _():
            own[h] = total

    barrier = pltpu.get_barrier_semaphore()
    peers = [core_peer, side_peer]
    peers += [far_peer(i) for i in range(1, blocks)]
    peers += [(me, lax.rem(hd + o, nh)) for o in range(1, nh)]
    for peer in peers:
        pl.semaphore_signal(barrier, inc=1, device_id=peer, device_id_type=MESH)
    for r in range(rows):
        for h in range(heads):
            q_t[r, h] = q_ref[r, h].T
            g_t[r, h] = g_ref[r, h].T
    pl.semaphore_wait(barrier, len(peers))

    for h in range(heads):
        bias_all[h, 0, side, core] = bias_ref[h]
    stage_far(0)

    def send_far(t):
        h, i = step_of(t)

        @pl.when(i != 0)
        def _():
            bias_far(h, i).start()

    ahead = min(AHEAD, steps)
    for t in range(ahead):
        send_far(jnp.int32(t))

    for r in range(rows):
        for h in range(heads):
            k_t[r, h] = k_ref[r, h].T
    dk_acc[...] = jnp.zeros_like(dk_acc)
    dv_acc[...] = jnp.zeros_like(dv_acc)
    stage_side(0)
    if steps > 1:
        stage_far(1)

    block = GROUP * j_own
    sub = min(block, 64)
    per_sub = sub // j_own if sub > j_own else 1
    sub = per_sub * j_own
    nn = (((1,), (0,)), ((), ()))
    tn = (((0,), (0,)), ((), ()))

    @pl.loop(0, steps)
    def _(t):
        h, i = step_of(t)

        @pl.when(t + ahead < steps)
        def _():
            send_far(t + ahead)

        @pl.when(t + 1 < steps)
        def _():
            stage_side(t + 1)

        stage_core(t)
        first = pl.multiple_of(xor(far, i, blocks) * block, block)

        @pl.loop(0, block // sub)
        def _(part):
            at = pl.multiple_of(part * sub, sub)
            pieces = []
            for u in range(per_sub):
                o = part * per_sub + u
                pieces.append(bias_all[h, i, lax.div(o, 2), lax.rem(o, 2)].astype(F32))
            b = pieces[0] if per_sub == 1 else jnp.concatenate(pieces, axis=0)
            total = None
            for r in range(rows):
                qb = q_t[r, h, pl.ds(first + at, sub), :]
                gb = g_t[r, h, pl.ds(first + at, sub), :]
                s = lax.dot_general(qb, k_ref[r, h], nn, preferred_element_type=F32) * scale + b
                e = jnp.exp(s - jnp.max(s, axis=-1, keepdims=True))
                inv = 1.0 / jnp.sum(e, axis=-1, keepdims=True)
                dp = lax.dot_general(gb, v_ref[r, h], nn, preferred_element_type=F32)
                p = e * inv
                delta = jnp.sum(p * dp, axis=-1, keepdims=True)
                ds = p * (dp - delta)
                p_low[r, pl.ds(at, sub), :] = p.astype(BF16)
                d_low[r, pl.ds(at, sub), :] = ds.astype(BF16)
                total = ds if total is None else total + ds
            for u in range(per_sub):
                o = part * per_sub + u
                d_blk[lax.div(o, 2), lax.rem(o, 2)] = total[u * j_own : (u + 1) * j_own]

        core_send[t] = d_blk[:, 1 - core].astype(BF16)
        sum_core(t).start()
        core_keep[t] = d_blk[:, core]

        @pl.when((t == 0) & (steps > 2))
        def _():
            stage_far(t + 2)

        @pl.when(t + 3 < steps)
        def _():
            stage_far(t + 3)

        for r in range(rows):
            qb = q_t[r, h, pl.ds(first, block), :]
            gb = g_t[r, h, pl.ds(first, block), :]
            dq_t[r, h, pl.ds(first, block), :] = lax.dot_general(d_low[r], k_t[r, h], nn, preferred_element_type=F32)
            dk_acc[r, h] += lax.dot_general(qb, d_low[r], tn, preferred_element_type=F32)
            dv_acc[r, h] += lax.dot_general(gb, p_low[r], tn, preferred_element_type=F32)

        reduce_core(t)

        @pl.when(t >= 1)
        def _():
            reduce_side(t - 1)

    def finish(h):
        @pl.loop(1, blocks)
        def _(i):
            sum_far(h, i).wait_recv()
            own[h] += far_recv[h, i].astype(F32)

        for y in range(nh):
            fin[y, h] = own[h, :, y * width : (y + 1) * width]
            fin_low[y, h] = own[h, :, y * width : (y + 1) * width].astype(BF16)
        for o in range(1, nh):
            head_copy(o, h).start()
        eh_ref[hd * heads + h] = fin[hd, h]

    for h in range(heads - 1):
        finish(h)
    for r in range(rows):
        for h in range(heads):
            dq_ref[r, h] = (dq_t[r, h] * scale).T.astype(BF16)
            dk_ref[r, h] = (dk_acc[r, h] * scale).astype(BF16)
            dv_ref[r, h] = dv_acc[r, h].astype(BF16)
    reduce_side(steps - 1)
    finish(heads - 1)
    for h in range(heads):
        for o in range(1, nh):
            copy = head_copy(o, h)
            copy.wait_recv()
            eh_ref[lax.rem(hd + nh - o, nh) * heads + h] = y_recv[o - 1, h].astype(F32)
            copy.wait_send()

    @pl.loop(0, steps)
    def _(t):
        h, i = step_of(t)
        bias_side(h, i).wait_send()
        bias_core_a(h, i).wait_send()
        bias_core_b(h, i).wait_send()
        sum_core(t).wait_send()
        sum_side(t).wait_send()

        @pl.when(i != 0)
        def _():
            bias_far(h, i).wait_send()
            sum_far(h, i).wait_send()


def attention(n, nh, q, k, v, g, bias):
    rows, heads, depth, length = q.shape
    j_own = length // n
    blocks = n // GROUP
    steps = heads * blocks
    block = GROUP * j_own
    width = length // nh
    dma = pltpu.SemaphoreType.DMA
    vm = pltpu.VMEM
    grid2 = (heads, blocks)
    return pl.pallas_call(
        functools.partial(attention_kernel, n, nh),
        out_shape=[jax.ShapeDtypeStruct(q.shape, BF16)] * 3
        + [jax.ShapeDtypeStruct((nh * heads, j_own, width), F32)],
        in_specs=[pl.BlockSpec(memory_space=pltpu.VMEM)] * 5,
        out_specs=[pl.BlockSpec(memory_space=pltpu.VMEM)] * 4,
        scratch_shapes=[
            vm((rows, heads, length, depth), BF16),
            vm((rows, heads, length, depth), BF16),
            vm((rows, heads, length, depth), BF16),
            vm((rows, heads, length, depth), F32),
            vm(q.shape, F32),
            vm(q.shape, F32),
            vm((rows, block, length), BF16),
            vm((rows, block, length), BF16),
            vm((2, 2, j_own, length), F32),
            vm(grid2 + (2, 2, j_own, length), BF16),
            vm((steps, 2, j_own, length), BF16),
            vm((steps, 2, j_own, length), F32),
            vm((steps, 2, j_own, length), BF16),
            vm((steps, j_own, length), BF16),
            vm((steps, j_own, length), F32),
            vm((steps, j_own, length), BF16),
            vm(grid2 + (j_own, length), BF16),
            vm(grid2 + (j_own, length), BF16),
            vm((heads, j_own, length), F32),
            vm((nh, heads, j_own, width), F32),
            vm((nh, heads, j_own, width), BF16),
            vm((max(nh - 1, 1), heads, j_own, width), BF16),
        ]
        + [dma(grid2)] * 8
        + [dma((steps,))] * 4
        + [dma(grid2)] * 2
        + [dma((max(nh - 1, 1), heads))] * 2,
        compiler_params=pltpu.CompilerParams(
            collective_id=0, has_side_effects=True, vmem_limit_bytes=56 * 1024 * 1024
        ),
        name="attention",
    )(q, k, v, g, bias)


def pair_kernel(d_ref, w_ref, q_in, k_in, v_in, q_out, k_out, v_out, out_ref, wide):
    heads, count, width = d_ref.shape
    channels = out_ref.shape[2]

    @pl.when(pl.program_id(0) == 0)
    def _():
        wide[...] = jnp.zeros_like(wide)
        for part in range(wide.shape[0] // (heads * count)):
            for h in range(heads):
                for j in range(count):
                    row = (part * heads + h) * count + j
                    wide[row : row + 1, j * channels : (j + 1) * channels] = w_ref[h : h + 1].astype(F32)
        q_out[...] = q_in[...]
        k_out[...] = k_in[...]
        v_out[...] = v_in[...]

    d = d_ref[...].reshape(heads * count, width)
    high = d.astype(BF16)
    rest = d - high.astype(F32)
    mid = rest.astype(BF16)
    low = (rest - mid.astype(F32)).astype(BF16)
    parts = jnp.concatenate([high, mid, low], axis=0)
    res = lax.dot_general(parts, wide[...].astype(BF16), (((0,), (0,)), ((), ())), preferred_element_type=F32)
    for j in range(count):
        out_ref[j] = res[:, j * channels : (j + 1) * channels].astype(BF16)


def pair(every_head, w_bias, grads):
    heads, j_own, width = every_head.shape
    channels = w_bias.shape[0]
    count = 8
    whole = pl.BlockSpec(grads[0].shape, lambda i: (0, 0, 0, 0))
    return pl.pallas_call(
        pair_kernel,
        grid=(j_own // count,),
        in_specs=[
            pl.BlockSpec((heads, count, width), lambda i: (0, i, 0)),
            pl.BlockSpec((heads, channels), lambda i: (0, 0)),
            whole,
            whole,
            whole,
        ],
        out_specs=[whole] * 3 + [pl.BlockSpec((count, width, channels), lambda i: (i, 0, 0))],
        out_shape=[jax.ShapeDtypeStruct(grads[0].shape, BF16)] * 3
        + [jax.ShapeDtypeStruct((j_own, width, channels), BF16)],
        scratch_shapes=[pltpu.VMEM((3 * heads * count, count * channels), F32)],
        name="pair",
    )(every_head, w_bias.T, *grads)


def solution(mesh):
    n, nh = mesh.shape["rows"], mesh.shape["heads"]

    def shards(queries, keys, values, d_out, bias, w_bias):
        dq, dk, dv, every_head = attention(n, nh, queries, keys, values, d_out, bias)
        return tuple(pair(every_head, w_bias, (dq, dk, dv)))

    spec = P("rows", "heads", None, None)
    return jax.shard_map(
        shards,
        mesh=mesh,
        in_specs=(spec, spec, spec, spec, P("heads", "rows", None), P()),
        out_specs=(spec, spec, spec, P("rows", "heads", None)),
        check_vma=False,
    )
```

```python
import functools

import jax
import jax.numpy as jnp
from jax import lax
from jax.experimental import pallas as pl
from jax.experimental.pallas import tpu as pltpu
from jax.sharding import PartitionSpec as P

MESH = pl.DeviceIdType.MESH
AHEAD = 4
GROUP = 4
BF16, F32 = jnp.bfloat16, jnp.float32


def xor(a, b, top):
    total, bit = 0, 1
    while bit < top:
        total = total + bit * lax.rem(lax.rem(lax.div(a, bit), 2) + lax.rem(lax.div(b, bit), 2), 2)
        bit *= 2
    return total


def attention_kernel(
    n, nh, q_ref, k_ref, v_ref, g_ref, bias_ref, dq_ref, dk_ref, dv_ref, eh_ref,
    q_t, g_t, k_t, dq_t, dk_acc, dv_acc, p_low, d_low, d_blk,
    bias_all, core_send, core_keep, core_recv, side_send, side_keep, side_recv,
    far_send, far_recv, own, fin, fin_low, y_recv,
    zs, zr, xs, xr, as_, ar, bs, br, cs, cr, ss, sr, fs, fr, ys, yr,
):
    rows, heads, depth, length = q_ref.shape
    j_own = length // n
    blocks = n // GROUP
    steps = heads * blocks
    width = length // nh
    scale = depth ** (-0.5)
    me, hd = lax.axis_index("rows"), lax.axis_index("heads")
    core = lax.rem(me, 2)
    side = lax.rem(lax.div(me, 2), 2)
    far = lax.div(me, GROUP)
    core_peer = (me + 1 - 2 * core, hd)
    side_peer = (me + 2 - 4 * side, hd)

    def far_peer(i):
        return (xor(far, i, blocks) * GROUP + lax.rem(me, GROUP), hd)

    def step_of(t):
        h = lax.div(t, blocks)
        i = lax.rem(t, blocks)
        return h, i + lax.rem(h, 2) * (blocks - 1 - 2 * i)

    def remote(src, dst, send, recv, device):
        return pltpu.make_async_remote_copy(
            src_ref=src, dst_ref=dst, send_sem=send, recv_sem=recv, device_id=device, device_id_type=MESH
        )

    def bias_far(h, i):
        return remote(bias_ref.at[h], bias_all.at[h, i, side, core], zs.at[h, i], zr.at[h, i], far_peer(i))

    def bias_side(h, i):
        spot = bias_all.at[h, i, side, core]
        return remote(spot, spot, xs.at[h, i], xr.at[h, i], side_peer)

    def bias_core_a(h, i):
        spot = bias_all.at[h, i, side, core]
        return remote(spot, spot, as_.at[h, i], ar.at[h, i], core_peer)

    def bias_core_b(h, i):
        spot = bias_all.at[h, i, 1 - side, core]
        return remote(spot, spot, bs.at[h, i], br.at[h, i], core_peer)

    def sum_core(t):
        return remote(core_send.at[t], core_recv.at[t], cs.at[t], cr.at[t], core_peer)

    def sum_side(t):
        return remote(side_send.at[t], side_recv.at[t], ss.at[t], sr.at[t], side_peer)

    def sum_far(h, i):
        return remote(far_send.at[h, i], far_recv.at[h, i], fs.at[h, i], fr.at[h, i], far_peer(i))

    def head_copy(o, h):
        to = lax.rem(hd + o, nh)
        return remote(fin_low.at[to, h], y_recv.at[o - 1, h], ys.at[o - 1, h], yr.at[o - 1, h], (me, to))

    def stage_far(t):
        h, i = step_of(t)

        @pl.when(i != 0)
        def _():
            bias_far(h, i).wait_recv()
            bias_side(h, i).start()
            bias_core_a(h, i).start()

    def stage_side(t):
        h, i = step_of(t)
        bias_side(h, i).wait_recv()
        bias_core_b(h, i).start()

    def stage_core(t):
        h, i = step_of(t)
        bias_core_a(h, i).wait_recv()
        bias_core_b(h, i).wait_recv()

    def reduce_core(t):
        sum_core(t).wait_recv()
        side_send[t] = (core_keep[t, 1 - side] + core_recv[t, 1 - side].astype(F32)).astype(BF16)
        sum_side(t).start()
        side_keep[t] = core_keep[t, side] + core_recv[t, side].astype(F32)

    def reduce_side(t):
        h, i = step_of(t)
        sum_side(t).wait_recv()
        total = side_keep[t] + side_recv[t].astype(F32)

        @pl.when(i != 0)
        def _():
            far_send[h, i] = total.astype(BF16)
            sum_far(h, i).start()

        @pl.when(i == 0)
        def _():
            own[h] = total

    barrier = pltpu.get_barrier_semaphore()
    peers = [core_peer, side_peer]
    peers += [far_peer(i) for i in range(1, blocks)]
    peers += [(me, lax.rem(hd + o, nh)) for o in range(1, nh)]
    for peer in peers:
        pl.semaphore_signal(barrier, inc=1, device_id=peer, device_id_type=MESH)
    for r in range(rows):
        for h in range(heads):
            q_t[r, h] = q_ref[r, h].T
            g_t[r, h] = g_ref[r, h].T
    pl.semaphore_wait(barrier, len(peers))

    for h in range(heads):
        bias_all[h, 0, side, core] = bias_ref[h]
    for h in range(heads):
        bias_side(h, 0).start()
        bias_core_a(h, 0).start()

    def send_far(t):
        h, i = step_of(t)

        @pl.when(i != 0)
        def _():
            bias_far(h, i).start()

    ahead = min(AHEAD, steps)
    for t in range(ahead):
        send_far(jnp.int32(t))

    for r in range(rows):
        for h in range(heads):
            k_t[r, h] = k_ref[r, h].T
    dk_acc[...] = jnp.zeros_like(dk_acc)
    dv_acc[...] = jnp.zeros_like(dv_acc)
    stage_side(0)
    if steps > 1:
        stage_far(1)

    block = GROUP * j_own
    sub = min(block, 64)
    per_sub = sub // j_own if sub > j_own else 1
    sub = per_sub * j_own
    nn = (((1,), (0,)), ((), ()))
    tn = (((0,), (0,)), ((), ()))

    @pl.loop(0, steps)
    def _(t):
        h, i = step_of(t)

        @pl.when(t + ahead < steps)
        def _():
            send_far(t + ahead)

        @pl.when(t + 1 < steps)
        def _():
            stage_side(t + 1)

        stage_core(t)
        first = pl.multiple_of(xor(far, i, blocks) * block, block)

        @pl.loop(0, block // sub)
        def _(part):
            at = pl.multiple_of(part * sub, sub)
            pieces = []
            for u in range(per_sub):
                o = part * per_sub + u
                pieces.append(bias_all[h, i, lax.div(o, 2), lax.rem(o, 2)].astype(F32))
            b = pieces[0] if per_sub == 1 else jnp.concatenate(pieces, axis=0)
            total = None
            for r in range(rows):
                qb = q_t[r, h, pl.ds(first + at, sub), :]
                gb = g_t[r, h, pl.ds(first + at, sub), :]
                s = lax.dot_general(qb, k_ref[r, h], nn, preferred_element_type=F32) * scale + b
                e = jnp.exp(s - jnp.max(s, axis=-1, keepdims=True))
                inv = 1.0 / jnp.sum(e, axis=-1, keepdims=True)
                dp = lax.dot_general(gb, v_ref[r, h], nn, preferred_element_type=F32)
                p = e * inv
                delta = jnp.sum(p * dp, axis=-1, keepdims=True)
                ds = p * (dp - delta)
                p_low[r, pl.ds(at, sub), :] = p.astype(BF16)
                d_low[r, pl.ds(at, sub), :] = ds.astype(BF16)
                total = ds if total is None else total + ds
            for u in range(per_sub):
                o = part * per_sub + u
                d_blk[lax.div(o, 2), lax.rem(o, 2)] = total[u * j_own : (u + 1) * j_own]

        core_send[t] = d_blk[:, 1 - core].astype(BF16)
        sum_core(t).start()
        core_keep[t] = d_blk[:, core]

        @pl.when((t == 0) & (steps > 2))
        def _():
            stage_far(t + 2)

        @pl.when(t + 3 < steps)
        def _():
            stage_far(t + 3)

        for r in range(rows):
            qb = q_t[r, h, pl.ds(first, block), :]
            gb = g_t[r, h, pl.ds(first, block), :]
            dq_t[r, h, pl.ds(first, block), :] = lax.dot_general(d_low[r], k_t[r, h], nn, preferred_element_type=F32)
            dk_acc[r, h] += lax.dot_general(qb, d_low[r], tn, preferred_element_type=F32)
            dv_acc[r, h] += lax.dot_general(gb, p_low[r], tn, preferred_element_type=F32)

        reduce_core(t)

        @pl.when(t >= 1)
        def _():
            reduce_side(t - 1)

    def finish(h):
        @pl.loop(1, blocks)
        def _(i):
            sum_far(h, i).wait_recv()
            own[h] += far_recv[h, i].astype(F32)

        for y in range(nh):
            fin[y, h] = own[h, :, y * width : (y + 1) * width]
            fin_low[y, h] = own[h, :, y * width : (y + 1) * width].astype(BF16)
        for o in range(1, nh):
            head_copy(o, h).start()
        eh_ref[hd * heads + h] = fin[hd, h]

    for h in range(heads - 1):
        finish(h)
    for r in range(rows):
        for h in range(heads):
            dq_ref[r, h] = (dq_t[r, h] * scale).T.astype(BF16)
            dk_ref[r, h] = (dk_acc[r, h] * scale).astype(BF16)
            dv_ref[r, h] = dv_acc[r, h].astype(BF16)
    reduce_side(steps - 1)
    finish(heads - 1)
    for h in range(heads):
        for o in range(1, nh):
            copy = head_copy(o, h)
            copy.wait_recv()
            eh_ref[lax.rem(hd + nh - o, nh) * heads + h] = y_recv[o - 1, h].astype(F32)
            copy.wait_send()

    @pl.loop(0, steps)
    def _(t):
        h, i = step_of(t)
        bias_side(h, i).wait_send()
        bias_core_a(h, i).wait_send()
        bias_core_b(h, i).wait_send()
        sum_core(t).wait_send()
        sum_side(t).wait_send()

        @pl.when(i != 0)
        def _():
            bias_far(h, i).wait_send()
            sum_far(h, i).wait_send()


def attention(n, nh, q, k, v, g, bias):
    rows, heads, depth, length = q.shape
    j_own = length // n
    blocks = n // GROUP
    steps = heads * blocks
    block = GROUP * j_own
    width = length // nh
    dma = pltpu.SemaphoreType.DMA
    vm = pltpu.VMEM
    grid2 = (heads, blocks)
    return pl.pallas_call(
        functools.partial(attention_kernel, n, nh),
        out_shape=[jax.ShapeDtypeStruct(q.shape, BF16)] * 3
        + [jax.ShapeDtypeStruct((nh * heads, j_own, width), F32)],
        in_specs=[pl.BlockSpec(memory_space=pltpu.VMEM)] * 5,
        out_specs=[pl.BlockSpec(memory_space=pltpu.VMEM)] * 4,
        scratch_shapes=[
            vm((rows, heads, length, depth), BF16),
            vm((rows, heads, length, depth), BF16),
            vm((rows, heads, length, depth), BF16),
            vm((rows, heads, length, depth), F32),
            vm(q.shape, F32),
            vm(q.shape, F32),
            vm((rows, block, length), BF16),
            vm((rows, block, length), BF16),
            vm((2, 2, j_own, length), F32),
            vm(grid2 + (2, 2, j_own, length), BF16),
            vm((steps, 2, j_own, length), BF16),
            vm((steps, 2, j_own, length), F32),
            vm((steps, 2, j_own, length), BF16),
            vm((steps, j_own, length), BF16),
            vm((steps, j_own, length), F32),
            vm((steps, j_own, length), BF16),
            vm(grid2 + (j_own, length), BF16),
            vm(grid2 + (j_own, length), BF16),
            vm((heads, j_own, length), F32),
            vm((nh, heads, j_own, width), F32),
            vm((nh, heads, j_own, width), BF16),
            vm((max(nh - 1, 1), heads, j_own, width), BF16),
        ]
        + [dma(grid2)] * 8
        + [dma((steps,))] * 4
        + [dma(grid2)] * 2
        + [dma((max(nh - 1, 1), heads))] * 2,
        compiler_params=pltpu.CompilerParams(
            collective_id=0, has_side_effects=True, vmem_limit_bytes=56 * 1024 * 1024
        ),
        name="attention",
    )(q, k, v, g, bias)


def pair_kernel(d_ref, w_ref, q_in, k_in, v_in, q_out, k_out, v_out, out_ref, wide):
    heads, count, width = d_ref.shape
    channels = out_ref.shape[2]

    @pl.when(pl.program_id(0) == 0)
    def _():
        wide[...] = jnp.zeros_like(wide)
        for part in range(wide.shape[0] // (heads * count)):
            for h in range(heads):
                for j in range(count):
                    row = (part * heads + h) * count + j
                    wide[row : row + 1, j * channels : (j + 1) * channels] = w_ref[h : h + 1].astype(F32)
        q_out[...] = q_in[...]
        k_out[...] = k_in[...]
        v_out[...] = v_in[...]

    d = d_ref[...].reshape(heads * count, width)
    high = d.astype(BF16)
    rest = d - high.astype(F32)
    mid = rest.astype(BF16)
    low = (rest - mid.astype(F32)).astype(BF16)
    parts = jnp.concatenate([high, mid, low], axis=0)
    res = lax.dot_general(parts, wide[...].astype(BF16), (((0,), (0,)), ((), ())), preferred_element_type=F32)
    for j in range(count):
        out_ref[j] = res[:, j * channels : (j + 1) * channels].astype(BF16)


def pair(every_head, w_bias, grads):
    heads, j_own, width = every_head.shape
    channels = w_bias.shape[0]
    count = min(16, j_own)
    whole = pl.BlockSpec(grads[0].shape, lambda i: (0, 0, 0, 0))
    return pl.pallas_call(
        pair_kernel,
        grid=(j_own // count,),
        in_specs=[
            pl.BlockSpec((heads, count, width), lambda i: (0, i, 0)),
            pl.BlockSpec((heads, channels), lambda i: (0, 0)),
            whole,
            whole,
            whole,
        ],
        out_specs=[whole] * 3 + [pl.BlockSpec((count, width, channels), lambda i: (i, 0, 0))],
        out_shape=[jax.ShapeDtypeStruct(grads[0].shape, BF16)] * 3
        + [jax.ShapeDtypeStruct((j_own, width, channels), BF16)],
        scratch_shapes=[pltpu.VMEM((3 * heads * count, count * channels), F32)],
        name="pair",
    )(every_head, w_bias.T, *grads)


def solution(mesh):
    n, nh = mesh.shape["rows"], mesh.shape["heads"]

    def shards(queries, keys, values, d_out, bias, w_bias):
        dq, dk, dv, every_head = attention(n, nh, queries, keys, values, d_out, bias)
        return tuple(pair(every_head, w_bias, (dq, dk, dv)))

    spec = P("rows", "heads", None, None)
    return jax.shard_map(
        shards,
        mesh=mesh,
        in_specs=(spec, spec, spec, spec, P("heads", "rows", None), P()),
        out_specs=(spec, spec, spec, P("rows", "heads", None)),
        check_vma=False,
    )
```
